32 devices in a mesh: groups: 2 (over x), row: 8 (over z, y), col: 2 (over core).
Axes of the slice: x: 2, y: 2, z: 4, core: 2. Of those that a mesh axis runs over, the one named last changes fastest.
Arguments:
- pair_repr: bfloat16 [64, 32, 128], P(('groups', 'row'), 'col'), parts along dimension 0, may hold values from -6 to 6
- in_gain: float32 [128], replicated, may hold values from 0.5 to 1.5
- in_bias: float32 [128], replicated, may hold values from -0.5 to 0.5
- left_gate_w: bfloat16 [128, 128], replicated, may hold values from -0.5 to 0.5
- left_w: bfloat16 [128, 128], replicated, may hold values from -0.5 to 0.5
- right_gate_w: bfloat16 [128, 128], replicated, may hold values from -0.5 to 0.5
- right_w: bfloat16 [128, 128], replicated, may hold values from -0.5 to 0.5
- out_gate_w: bfloat16 [128, 128], replicated, may hold values from -0.5 to 0.5
- mid_gain: float32 [128], replicated, may hold values from 0.5 to 1.5
- mid_bias: float32 [128], replicated, may hold values from -0.5 to 0.5
- out_w: bfloat16 [128, 128], replicated, may hold values from -0.5 to 0.5
Outputs:
- update: bfloat16 [64, 32, 128], P(('groups', 'row'), 'col'), parts along dimension 0
The draws below stay inside these ranges and needn't reach their ends.
There are 2 independent parts, one for each index of `groups`. The reference program is written for one: setup_inputs(seed, part) draws one part's arguments, and reference() takes and returns one part's arrays. A program takes and returns all parts, laid end to end along the dimension named above; an argument that names none is the same for every part. Nothing has to cross between parts.
All inputs are finite; a program needn't handle non-finite values.
Results may differ from the reference program's by a relative error of at most 0.015.
Values may be sent and summed in bfloat16 or wider, within the bound.
A program may use at most 64 MiB of HBM per device.

```python
import jax
import jax.numpy as jnp
from jax import lax

C = 128
HID = 128
TOKENS = 32


def steps_of(own_key, dims, split, smallest, largest):
    def one(position, shards_of):
        draws = jax.random.uniform(jax.random.fold_in(jax.random.fold_in(own_key, 6), position), (shards_of,), jnp.float32, smallest / len(split), largest / len(split))
        return jnp.repeat(jnp.exp(draws), dims[position] // shards_of).reshape((-1,) + (1,) * (len(dims) - position - 1))

    factor_of = one(*split[0])
    for cut in split[1:]:
        factor_of = factor_of * one(*cut)
    return factor_of


def scatter_about(rng, extent, deviation, limit, shards=(), kind=jnp.bfloat16):
    gain = steps_of(rng, extent, shards, -0.22, 0.18) if shards else 1.0
    values = jax.random.normal(rng, extent, jnp.float32) * deviation * gain
    return jnp.minimum(jnp.maximum(values, -limit), limit).astype(kind)


def setup_inputs(seed: int = 0, part: int = 0) -> dict:
    keys = jax.random.split(jax.random.key(seed), 12)
    own_keys = jax.random.split(jax.random.fold_in(keys[11], part), 12)
    pair_repr = scatter_about(own_keys[0], (TOKENS, TOKENS, C), 1.0, 6.0, ((0, 8), (1, 2)))
    in_gain = jnp.clip(1.0 + 0.1 * jax.random.normal(keys[1], (C,), jnp.float32), 0.5, 1.5)
    in_bias = jnp.clip(jax.random.uniform(keys[2], (C,), jnp.float32, -0.5, 0.5), -0.5, 0.5)
    left_gate_w = scatter_about(keys[3], (C, HID), C ** -0.5, 0.5)
    left_w = scatter_about(keys[4], (C, HID), C ** -0.5, 0.5)
    right_gate_w = scatter_about(keys[5], (C, HID), C ** -0.5, 0.5)
    right_w = scatter_about(keys[6], (C, HID), C ** -0.5, 0.5)
    out_gate_w = scatter_about(keys[7], (C, C), C ** -0.5, 0.5)
    mid_gain = jnp.clip(1.0 + 0.1 * jax.random.normal(keys[8], (HID,), jnp.float32), 0.5, 1.5)
    mid_bias = jnp.clip(jax.random.uniform(keys[9], (HID,), jnp.float32, -0.5, 0.5), -0.5, 0.5)
    out_w = scatter_about(keys[10], (HID, C), HID ** -0.5, 0.5)
    return dict(pair_repr=pair_repr, in_gain=in_gain, in_bias=in_bias, left_gate_w=left_gate_w, left_w=left_w, right_gate_w=right_gate_w, right_w=right_w, out_gate_w=out_gate_w, mid_gain=mid_gain, mid_bias=mid_bias, out_w=out_w)


def layer_norm(values, norm_gain, norm_bias):
    average = lax.optimization_barrier(jnp.mean(values, axis=-1, keepdims=True))
    centred = values - average
    variance = lax.optimization_barrier(jnp.mean(centred * centred, axis=-1, keepdims=True))
    return centred / jnp.sqrt(variance + 1e-05) * norm_gain + norm_bias

def reference(pair_repr, in_gain, in_bias, left_gate_w, left_w, right_gate_w, right_w, out_gate_w, mid_gain, mid_bias, out_w):
    normed = layer_norm(pair_repr.astype(jnp.float32), in_gain, in_bias).astype(jnp.bfloat16)
    flattened = normed.reshape(TOKENS * TOKENS, C)
    left_side = (jax.nn.sigmoid(jnp.dot(flattened, left_gate_w, preferred_element_type=jnp.float32)) * jnp.dot(flattened, left_w, preferred_element_type=jnp.float32)).astype(jnp.bfloat16)
    right_side = (jax.nn.sigmoid(jnp.dot(flattened, right_gate_w, preferred_element_type=jnp.float32)) * jnp.dot(flattened, right_w, preferred_element_type=jnp.float32)).astype(jnp.bfloat16)
    gating = jax.nn.sigmoid(jnp.dot(flattened, out_gate_w, preferred_element_type=jnp.float32))
    left_side = left_side.reshape(TOKENS, TOKENS, HID).astype(jnp.float32)
    right_side = right_side.reshape(TOKENS, TOKENS, HID).astype(jnp.float32)
    triangle = jnp.einsum('ikh,jkh->ijh', left_side, right_side)
    middle = layer_norm(triangle, mid_gain, mid_bias).astype(jnp.bfloat16).reshape(TOKENS * TOKENS, HID)
    result = gating * jnp.dot(middle, out_w, preferred_element_type=jnp.float32)
    return result.astype(jnp.bfloat16).reshape(TOKENS, TOKENS, C)
```

```python
import functools

import jax
import jax.numpy as jnp
from jax import lax
from jax.experimental import pallas as pl
from jax.experimental.pallas import tpu as pltpu
from jax.sharding import PartitionSpec as P

MESH = pl.DeviceIdType.MESH


def normalise(values, gain, bias):
    average = jnp.mean(values, axis=-1, keepdims=True)
    centred = values - average
    variance = jnp.mean(centred * centred, axis=-1, keepdims=True)
    return centred * lax.rsqrt(variance + 1e-05) * gain + bias


def loop(count, body):
    if count <= 8:
        for step in range(count):
            body(step)
    else:

        def wrapped(step, carry):
            body(step)
            return carry

        lax.fori_loop(0, count, wrapped, 0)


def kernel(
    rows,
    pair_hbm,
    in_gain_hbm,
    in_bias_hbm,
    left_gate_hbm,
    left_hbm,
    right_gate_hbm,
    right_hbm,
    out_gate_hbm,
    mid_gain_hbm,
    mid_bias_hbm,
    out_hbm,
    result_ref,
    pair,
    weights,
    vectors,
    own_right,
    right_all,
    left_both,
    triangle,
    load_sem,
    send_sem,
    recv_sem,
    left_send_sem,
    left_recv_sem,
):
    row = lax.axis_index("row")
    col = lax.axis_index("col")
    row_count, col_count, channels = pair.shape
    blocks = col_count // row_count
    flat = row_count * col_count
    owner = row // blocks
    slot = row % blocks
    mine = owner == col

    sources = [
        (pair_hbm, pair),
        (in_gain_hbm, vectors.at[0]),
        (in_bias_hbm, vectors.at[1]),
        (right_gate_hbm, weights.at[0]),
        (right_hbm, weights.at[1]),
        (left_gate_hbm, weights.at[2]),
        (left_hbm, weights.at[3]),
        (out_gate_hbm, weights.at[4]),
        (out_hbm, weights.at[5]),
        (mid_gain_hbm, vectors.at[2]),
        (mid_bias_hbm, vectors.at[3]),
    ]
    loads = [
        pltpu.make_async_copy(source, target, load_sem.at[index])
        for index, (source, target) in enumerate(sources)
    ]
    for load in loads:
        load.start()

    barrier = pltpu.get_barrier_semaphore()

    def greet(step):
        other_row = col * blocks + step // 2
        other_col = step % 2

        @pl.when(jnp.logical_or(other_row != row, other_col != col))
        def _():
            pl.semaphore_signal(
                barrier, 1, device_id={"row": other_row, "col": other_col}, device_id_type=MESH
            )

    loop(2 * blocks, greet)

    @pl.when(jnp.logical_not(mine))
    def _():
        pl.semaphore_signal(barrier, 1, device_id={"row": row, "col": 1 - col}, device_id_type=MESH)

    for load in loads[:5]:
        load.wait()
    normed = normalise(
        pair[...].reshape(flat, channels).astype(jnp.float32), vectors[0], vectors[1]
    ).astype(jnp.bfloat16)

    def project(index):
        return jnp.dot(normed, weights[index], preferred_element_type=jnp.float32)

    def gated(gate, value):
        product = jax.nn.sigmoid(project(gate)) * project(value)
        return product.astype(jnp.bfloat16).reshape(row_count, col_count, channels)

    right_block = gated(0, 1)
    own_right[...] = right_block

    @pl.when(mine)
    def _():
        right_all[slot, col] = right_block

    pl.semaphore_wait(barrier, rows)

    def right_copy(offset):
        return pltpu.make_async_remote_copy(
            src_ref=own_right,
            dst_ref=right_all.at[slot, col],
            send_sem=send_sem.at[offset],
            recv_sem=recv_sem.at[slot, col],
            device_id={"row": lax.rem(row + offset, rows), "col": owner},
            device_id_type=MESH,
        )

    loop(rows - 1, lambda step: right_copy(step + 1).start())

    @pl.when(jnp.logical_not(mine))
    def _():
        right_copy(0).start()

    for load in loads[5:]:
        load.wait()
    left_both[col] = gated(2, 3)
    left_copy = pltpu.make_async_remote_copy(
        src_ref=left_both.at[col],
        dst_ref=left_both.at[col],
        send_sem=left_send_sem,
        recv_sem=left_recv_sem,
        device_id={"row": row, "col": 1 - col},
        device_id_type=MESH,
    )
    left_copy.start()
    gating = jax.nn.sigmoid(project(4))

    left_copy.wait_recv()

    def block_wait(step):
        block = step // 2
        half = step % 2

        @pl.when(jnp.logical_or(col * blocks + block != row, half != col))
        def _():
            pltpu.make_async_remote_copy(
                src_ref=own_right,
                dst_ref=right_all.at[block, half],
                send_sem=send_sem.at[0],
                recv_sem=recv_sem.at[block, half],
                device_id={"row": row, "col": 1 - col},
                device_id_type=MESH,
            ).wait_recv()

    def contract(block):
        for j in range(row_count):
            right0 = right_all[block, 0, j].astype(jnp.float32)
            right1 = right_all[block, 1, j].astype(jnp.float32)
            for i in range(row_count):
                terms = (
                    left_both[0, i].astype(jnp.float32) * right0
                    + left_both[1, i].astype(jnp.float32) * right1
                )
                triangle[i, pl.ds(block * row_count + j, 1), :] = jnp.sum(
                    terms, axis=0, keepdims=True
                )

    loop(2 * blocks, block_wait)
    loop(blocks, contract)

    middle = normalise(triangle[...].reshape(flat, channels), vectors[2], vectors[3])
    update = gating * jnp.dot(
        middle.astype(jnp.bfloat16), weights[5], preferred_element_type=jnp.float32
    )
    result_ref[...] = update.astype(jnp.bfloat16).reshape(row_count, col_count, channels)

    left_copy.wait_send()
    loop(rows - 1, lambda step: right_copy(step + 1).wait_send())

    @pl.when(jnp.logical_not(mine))
    def _():
        right_copy(0).wait_send()


def solution(mesh):
    rows = mesh.shape["row"]

    def on_device(pair_repr, in_gain, in_bias, left_gate_w, left_w, right_gate_w, right_w, out_gate_w, mid_gain, mid_bias, out_w):
        row_count, col_count, channels = pair_repr.shape
        blocks = col_count // row_count
        hbm = pl.BlockSpec(memory_space=pltpu.HBM)
        return pl.pallas_call(
            functools.partial(kernel, rows),
            out_shape=jax.ShapeDtypeStruct(pair_repr.shape, jnp.bfloat16),
            in_specs=[hbm] * 11,
            out_specs=pl.BlockSpec(memory_space=pltpu.VMEM),
            scratch_shapes=[
                pltpu.VMEM(pair_repr.shape, jnp.bfloat16),
                pltpu.VMEM((6, channels, channels), jnp.bfloat16),
                pltpu.VMEM((4, 1, channels), jnp.float32),
                pltpu.VMEM(pair_repr.shape, jnp.bfloat16),
                pltpu.VMEM((blocks, 2, row_count, col_count, channels), jnp.bfloat16),
                pltpu.VMEM((2, row_count, col_count, channels), jnp.bfloat16),
                pltpu.VMEM((row_count, col_count, channels), jnp.float32),
                pltpu.SemaphoreType.DMA((11,)),
                pltpu.SemaphoreType.DMA((rows,)),
                pltpu.SemaphoreType.DMA((blocks, 2)),
                pltpu.SemaphoreType.DMA,
                pltpu.SemaphoreType.DMA,
            ],
            compiler_params=pltpu.CompilerParams(
                collective_id=0, has_side_effects=True, vmem_limit_bytes=48 * 1024 * 1024
            ),
        )(
            pair_repr,
            in_gain.reshape(1, channels),
            in_bias.reshape(1, channels),
            left_gate_w,
            left_w,
            right_gate_w,
            right_w,
            out_gate_w,
            mid_gain.reshape(1, channels),
            mid_bias.reshape(1, channels),
            out_w,
        )

    in_specs = (P(("groups", "row"), "col", None),) + (P(),) * 10
    out_specs = P(("groups", "row"), "col", None)
    return jax.shard_map(
        on_device, mesh=mesh, in_specs=in_specs, out_specs=out_specs, check_vma=False
    )
```

```python
import functools

import jax
import jax.numpy as jnp
from jax import lax
from jax.experimental import pallas as pl
from jax.experimental.pallas import tpu as pltpu
from jax.sharding import PartitionSpec as P

MESH = pl.DeviceIdType.MESH


def normalise(values, gain, bias):
    average = jnp.mean(values, axis=-1, keepdims=True)
    centred = values - average
    variance = jnp.mean(centred * centred, axis=-1, keepdims=True)
    return centred * lax.rsqrt(variance + 1e-05) * gain + bias


def loop(count, body):
    if count <= 8:
        for step in range(count):
            body(step)
    else:

        def wrapped(step, carry):
            body(step)
            return carry

        lax.fori_loop(0, count, wrapped, 0)


def kernel(
    rows,
    pair_hbm,
    in_gain_hbm,
    in_bias_hbm,
    left_gate_hbm,
    left_hbm,
    right_gate_hbm,
    right_hbm,
    out_gate_hbm,
    mid_gain_hbm,
    mid_bias_hbm,
    out_hbm,
    result_ref,
    pair,
    weights,
    vectors,
    own_right,
    right_all,
    left_both,
    triangle,
    load_sem,
    send_sem,
    recv_sem,
    left_send_sem,
    left_recv_sem,
):
    row = lax.axis_index("row")
    col = lax.axis_index("col")
    row_count, col_count, channels = pair.shape
    blocks = col_count // row_count
    flat = row_count * col_count
    owner = row // blocks
    slot = row % blocks
    mine = owner == col

    sources = [
        (pair_hbm, pair),
        (in_gain_hbm, vectors.at[0]),
        (in_bias_hbm, vectors.at[1]),
        (right_gate_hbm, weights.at[0]),
        (right_hbm, weights.at[1]),
        (left_gate_hbm, weights.at[2]),
        (left_hbm, weights.at[3]),
        (out_gate_hbm, weights.at[4]),
        (out_hbm, weights.at[5]),
        (mid_gain_hbm, vectors.at[2]),
        (mid_bias_hbm, vectors.at[3]),
    ]
    loads = [
        pltpu.make_async_copy(source, target, load_sem.at[index])
        for index, (source, target) in enumerate(sources)
    ]
    for load in loads:
        load.start()

    barrier = pltpu.get_barrier_semaphore()

    def greet(step):
        other_row = col * blocks + step // 2
        other_col = step % 2

        @pl.when(jnp.logical_or(other_row != row, other_col != col))
        def _():
            pl.semaphore_signal(
                barrier, 1, device_id={"row": other_row, "col": other_col}, device_id_type=MESH
            )

    loop(2 * blocks, greet)

    @pl.when(jnp.logical_not(mine))
    def _():
        pl.semaphore_signal(barrier, 1, device_id={"row": row, "col": 1 - col}, device_id_type=MESH)

    for load in loads[:5]:
        load.wait()
    normed = normalise(
        pair[...].reshape(flat, channels).astype(jnp.float32), vectors[0], vectors[1]
    ).astype(jnp.bfloat16)

    def project(index):
        return jnp.dot(normed, weights[index], preferred_element_type=jnp.float32)

    def gated(gate, value):
        product = jax.nn.sigmoid(project(gate)) * project(value)
        return product.astype(jnp.bfloat16).reshape(row_count, col_count, channels)

    right_block = gated(0, 1)
    own_right[...] = right_block

    @pl.when(mine)
    def _():
        right_all[slot, col] = right_block

    pl.semaphore_wait(barrier, rows)

    def right_copy(offset):
        return pltpu.make_async_remote_copy(
            src_ref=own_right,
            dst_ref=right_all.at[slot, col],
            send_sem=send_sem.at[offset],
            recv_sem=recv_sem.at[slot, col],
            device_id={"row": lax.rem(row + offset, rows), "col": owner},
            device_id_type=MESH,
        )

    loop(rows - 1, lambda step: right_copy(step + 1).start())

    @pl.when(jnp.logical_not(mine))
    def _():
        right_copy(0).start()

    for load in loads[5:]:
        load.wait()
    left_both[col] = gated(2, 3)
    left_copy = pltpu.make_async_remote_copy(
        src_ref=left_both.at[col],
        dst_ref=left_both.at[col],
        send_sem=left_send_sem,
        recv_sem=left_recv_sem,
        device_id={"row": row, "col": 1 - col},
        device_id_type=MESH,
    )
    left_copy.start()
    gating = jax.nn.sigmoid(project(4))

    left_copy.wait_recv()

    def block_wait(step):
        block = step // 2
        half = step % 2

        @pl.when(jnp.logical_or(col * blocks + block != row, half != col))
        def _():
            pltpu.make_async_remote_copy(
                src_ref=own_right,
                dst_ref=right_all.at[block, half],
                send_sem=send_sem.at[0],
                recv_sem=recv_sem.at[block, half],
                device_id={"row": row, "col": 1 - col},
                device_id_type=MESH,
            ).wait_recv()

    def contract(block):
        for j in range(row_count):
            right0 = right_all[block, 0, j].astype(jnp.float32)
            right1 = right_all[block, 1, j].astype(jnp.float32)
            for i in range(row_count):
                terms = (
                    left_both[0, i].astype(jnp.float32) * right0
                    + left_both[1, i].astype(jnp.float32) * right1
                )
                triangle[i, pl.ds(block * row_count + j, 1), :] = jnp.sum(
                    terms, axis=0, keepdims=True
                )

    loop(2 * blocks, block_wait)
    loop(blocks, contract)

    middle = normalise(triangle[...].reshape(flat, channels), vectors[2], vectors[3])
    update = gating * jnp.dot(
        middle.astype(jnp.bfloat16), weights[5], preferred_element_type=jnp.float32
    )
    result_ref[...] = update.astype(jnp.bfloat16).reshape(row_count, col_count, channels)

    left_copy.wait_send()
    loop(rows - 1, lambda step: right_copy(step + 1).wait_send())

    @pl.when(jnp.logical_not(mine))
    def _():
        right_copy(0).wait_send()


def solution(mesh):
    rows = mesh.shape["row"]

    def on_device(pair_repr, in_gain, in_bias, left_gate_w, left_w, right_gate_w, right_w, out_gate_w, mid_gain, mid_bias, out_w):
        row_count, col_count, channels = pair_repr.shape
        blocks = col_count // row_count
        hbm = pl.BlockSpec(memory_space=pltpu.HBM)
        return pl.pallas_call(
            functools.partial(kernel, rows),
            out_shape=jax.ShapeDtypeStruct(pair_repr.shape, jnp.bfloat16),
            in_specs=[hbm] * 11,
            out_specs=pl.BlockSpec(memory_space=pltpu.VMEM),
            scratch_shapes=[
                pltpu.VMEM(pair_repr.shape, jnp.bfloat16),
                pltpu.VMEM((6, channels, channels), jnp.bfloat16),
                pltpu.VMEM((4, 1, channels), jnp.float32),
                pltpu.VMEM(pair_repr.shape, jnp.bfloat16),
                pltpu.VMEM((blocks, 2, row_count, col_count, channels), jnp.bfloat16),
                pltpu.VMEM((2, row_count, col_count, channels), jnp.bfloat16),
                pltpu.VMEM((row_count, col_count, channels), jnp.float32),
                pltpu.SemaphoreType.DMA((11,)),
                pltpu.SemaphoreType.DMA((rows,)),
                pltpu.SemaphoreType.DMA((blocks, 2)),
                pltpu.SemaphoreType.DMA,
                pltpu.SemaphoreType.DMA,
            ],
            compiler_params=pltpu.CompilerParams(
                collective_id=0, has_side_effects=True
            ),
        )(
            pair_repr,
            in_gain.reshape(1, channels),
            in_bias.reshape(1, channels),
            left_gate_w,
            left_w,
            right_gate_w,
            right_w,
            out_gate_w,
            mid_gain.reshape(1, channels),
            mid_bias.reshape(1, channels),
            out_w,
        )

    in_specs = (P(("groups", "row"), "col", None),) + (P(),) * 10
    out_specs = P(("groups", "row"), "col", None)
    return jax.shard_map(
        on_device, mesh=mesh, in_specs=in_specs, out_specs=out_specs, check_vma=False
    )
```

```python
import functools

import jax
import jax.numpy as jnp
from jax import lax
from jax.experimental import pallas as pl
from jax.experimental.pallas import tpu as pltpu
from jax.sharding import PartitionSpec as P

MESH = pl.DeviceIdType.MESH


def normalise(values, gain, bias):
    average = jnp.mean(values, axis=-1, keepdims=True)
    centred = values - average
    variance = jnp.mean(centred * centred, axis=-1, keepdims=True)
    return centred * lax.rsqrt(variance + 1e-05) * gain + bias


def loop(count, body):
    if count <= 8:
        for step in range(count):
            body(step)
    else:

        def wrapped(step, carry):
            body(step)
            return carry

        lax.fori_loop(0, count, wrapped, 0)


def kernel(
    rows,
    pair_hbm,
    in_gain_hbm,
    in_bias_hbm,
    left_gate_hbm,
    left_hbm,
    right_gate_hbm,
    right_hbm,
    out_gate_hbm,
    mid_gain_hbm,
    mid_bias_hbm,
    out_hbm,
    result_ref,
    pair,
    weights,
    vectors,
    own_right,
    right_all,
    left_both,
    triangle,
    load_sem,
    send_sem,
    recv_sem,
    left_send_sem,
    left_recv_sem,
):
    row = lax.axis_index("row")
    col = lax.axis_index("col")
    row_count, col_count, channels = pair.shape
    blocks = col_count // row_count
    flat = row_count * col_count
    owner = row // blocks
    slot = row % blocks
    mine = owner == col

    sources = [
        (pair_hbm, pair),
        (in_gain_hbm, vectors.at[0]),
        (in_bias_hbm, vectors.at[1]),
        (right_gate_hbm, weights.at[0]),
        (right_hbm, weights.at[1]),
        (left_gate_hbm, weights.at[2]),
        (left_hbm, weights.at[3]),
        (out_gate_hbm, weights.at[4]),
        (out_hbm, weights.at[5]),
        (mid_gain_hbm, vectors.at[2]),
        (mid_bias_hbm, vectors.at[3]),
    ]
    loads = [
        pltpu.make_async_copy(source, target, load_sem.at[index])
        for index, (source, target) in enumerate(sources)
    ]
    for load in loads:
        load.start()

    barrier = pltpu.get_barrier_semaphore()

    def greet(step):
        other_row = col * blocks + step // 2
        other_col = step % 2

        @pl.when(jnp.logical_or(other_row != row, other_col != col))
        def _():
            pl.semaphore_signal(
                barrier, 1, device_id={"row": other_row, "col": other_col}, device_id_type=MESH
            )

    loop(2 * blocks, greet)

    @pl.when(jnp.logical_not(mine))
    def _():
        pl.semaphore_signal(barrier, 1, device_id={"row": row, "col": 1 - col}, device_id_type=MESH)

    for load in loads[:5]:
        load.wait()
    normed = normalise(
        pair[...].reshape(flat, channels).astype(jnp.float32), vectors[0], vectors[1]
    ).astype(jnp.bfloat16)

    def project(index):
        return jnp.dot(normed, weights[index], preferred_element_type=jnp.float32)

    def gated(gate, value):
        product = jax.nn.sigmoid(project(gate)) * project(value)
        return product.astype(jnp.bfloat16).reshape(row_count, col_count, channels)

    right_block = gated(0, 1)
    own_right[...] = right_block

    @pl.when(mine)
    def _():
        right_all[slot, col] = right_block

    pl.semaphore_wait(barrier, rows)

    def right_copy(offset):
        return pltpu.make_async_remote_copy(
            src_ref=own_right,
            dst_ref=right_all.at[slot, col],
            send_sem=send_sem.at[offset],
            recv_sem=recv_sem.at[slot, col],
            device_id={"row": lax.rem(row + offset, rows), "col": owner},
            device_id_type=MESH,
        )

    loop(rows - 1, lambda step: right_copy(step + 1).start())

    @pl.when(jnp.logical_not(mine))
    def _():
        right_copy(0).start()

    for load in loads[5:]:
        load.wait()
    left_both[col] = gated(2, 3)
    left_copy = pltpu.make_async_remote_copy(
        src_ref=left_both.at[col],
        dst_ref=left_both.at[col],
        send_sem=left_send_sem,
        recv_sem=left_recv_sem,
        device_id={"row": row, "col": 1 - col},
        device_id_type=MESH,
    )
    left_copy.start()
    gating = jax.nn.sigmoid(project(4))

    left_copy.wait_recv()

    def block_wait(step):
        block = step // 2
        half = step % 2

        @pl.when(jnp.logical_or(col * blocks + block != row, half != col))
        def _():
            pltpu.make_async_remote_copy(
                src_ref=own_right,
                dst_ref=right_all.at[block, half],
                send_sem=send_sem.at[0],
                recv_sem=recv_sem.at[block, half],
                device_id={"row": row, "col": 1 - col},
                device_id_type=MESH,
            ).wait_recv()

    def contract(block):
        for j in range(row_count):
            right0 = right_all[block, 0, j].astype(jnp.float32)
            right1 = right_all[block, 1, j].astype(jnp.float32)
            for i in range(row_count):
                terms = (
                    left_both[0, i].astype(jnp.float32) * right0
                    + left_both[1, i].astype(jnp.float32) * right1
                )
                triangle[i, pl.ds(block * row_count + j, 1), :] = jnp.sum(
                    terms, axis=0, keepdims=True
                )

    loop(2 * blocks, block_wait)
    loop(blocks, contract)

    middle = normalise(triangle[...].reshape(flat, channels), vectors[2], vectors[3])
    update = gating * jnp.dot(
        middle.astype(jnp.bfloat16), weights[5], preferred_element_type=jnp.float32
    )
    result_ref[...] = update.astype(jnp.bfloat16).reshape(row_count, col_count, channels)

    left_copy.wait_send()
    loop(rows - 1, lambda step: right_copy(step + 1).wait_send())

    @pl.when(jnp.logical_not(mine))
    def _():
        right_copy(0).wait_send()


def solution(mesh):
    rows = mesh.shape["row"]

    def on_device(pair_repr, in_gain, in_bias, left_gate_w, left_w, right_gate_w, right_w, out_gate_w, mid_gain, mid_bias, out_w):
        row_count, col_count, channels = pair_repr.shape
        blocks = col_count // row_count
        hbm = pl.BlockSpec(memory_space=pltpu.HBM)
        return pl.pallas_call(
            functools.partial(kernel, rows),
            out_shape=pltpu.VMEM(pair_repr.shape, jnp.bfloat16),
            in_specs=[hbm] * 11,
            out_specs=pl.BlockSpec(memory_space=pltpu.VMEM),
            scratch_shapes=[
                pltpu.VMEM(pair_repr.shape, jnp.bfloat16),
                pltpu.VMEM((6, channels, channels), jnp.bfloat16),
                pltpu.VMEM((4, 1, channels), jnp.float32),
                pltpu.VMEM(pair_repr.shape, jnp.bfloat16),
                pltpu.VMEM((blocks, 2, row_count, col_count, channels), jnp.bfloat16),
                pltpu.VMEM((2, row_count, col_count, channels), jnp.bfloat16),
                pltpu.VMEM((row_count, col_count, channels), jnp.float32),
                pltpu.SemaphoreType.DMA((11,)),
                pltpu.SemaphoreType.DMA((rows,)),
                pltpu.SemaphoreType.DMA((blocks, 2)),
                pltpu.SemaphoreType.DMA,
                pltpu.SemaphoreType.DMA,
            ],
            compiler_params=pltpu.CompilerParams(
                collective_id=0, has_side_effects=True
            ),
        )(
            pair_repr,
            in_gain.reshape(1, channels),
            in_bias.reshape(1, channels),
            left_gate_w,
            left_w,
            right_gate_w,
            right_w,
            out_gate_w,
            mid_gain.reshape(1, channels),
            mid_bias.reshape(1, channels),
            out_w,
        )

    in_specs = (P(("groups", "row"), "col", None),) + (P(),) * 10
    out_specs = P(("groups", "row"), "col", None)
    return jax.shard_map(
        on_device, mesh=mesh, in_specs=in_specs, out_specs=out_specs, check_vma=False
    )
```

```python
import functools

import jax
import jax.numpy as jnp
from jax import lax
from jax.experimental import pallas as pl
from jax.experimental.pallas import tpu as pltpu
from jax.sharding import PartitionSpec as P

MESH = pl.DeviceIdType.MESH


def normalise(values, gain, bias):
    average = jnp.mean(values, axis=-1, keepdims=True)
    centred = values - average
    variance = jnp.mean(centred * centred, axis=-1, keepdims=True)
    return centred * lax.rsqrt(variance + 1e-05) * gain + bias


def loop(count, body):
    if count <= 16:
        for step in range(count):
            body(step)
    else:

        def wrapped(step, carry):
            body(step)
            return carry

        lax.fori_loop(0, count, wrapped, 0)


def kernel(
    rows,
    pair_hbm,
    in_gain_hbm,
    in_bias_hbm,
    left_gate_hbm,
    left_hbm,
    right_gate_hbm,
    right_hbm,
    out_gate_hbm,
    mid_gain_hbm,
    mid_bias_hbm,
    out_hbm,
    result_ref,
    pair,
    weights,
    vectors,
    own_right,
    right_all,
    left_both,
    triangle,
    load_sem,
    send_sem,
    recv_sem,
    left_send_sem,
    left_recv_sem,
    ready_sem,
    left_ready_sem,
):
    row = lax.axis_index("row")
    col = lax.axis_index("col")
    row_count, col_count, channels = pair.shape
    blocks = col_count // row_count
    flat = row_count * col_count
    owner = row // blocks
    slot = row % blocks
    mine = owner == col

    sources = [
        (pair_hbm, pair),
        (in_gain_hbm, vectors.at[0]),
        (in_bias_hbm, vectors.at[1]),
        (right_gate_hbm, weights.at[0]),
        (right_hbm, weights.at[1]),
        (left_gate_hbm, weights.at[2]),
        (left_hbm, weights.at[3]),
        (out_gate_hbm, weights.at[4]),
        (out_hbm, weights.at[5]),
        (mid_gain_hbm, vectors.at[2]),
        (mid_bias_hbm, vectors.at[3]),
    ]
    loads = [
        pltpu.make_async_copy(source, target, load_sem.at[index])
        for index, (source, target) in enumerate(sources)
    ]
    for load in loads:
        load.start()

    rank = 2 * row + col
    barrier = pltpu.get_barrier_semaphore()

    def is_peer(other_row, other_col):
        return (other_col == owner) | (other_row // blocks == col) | (other_row == row)

    def greet(step):
        @pl.when(is_peer(step // 2, step % 2) & (step > rank))
        def _():
            pl.semaphore_signal(
                barrier, 1, device_id={"row": step // 2, "col": step % 2}, device_id_type=MESH
            )

    loop(2 * rows, greet)

    def count_lower(step, total):
        return total + jnp.where(is_peer(step // 2, step % 2) & (step < rank), 1, 0)

    lower = jnp.int32(0)
    if rows <= 8:
        for step in range(2 * rows):
            lower = count_lower(step, lower)
    else:
        lower = lax.fori_loop(0, 2 * rows, count_lower, lower)

    @pl.when(lower > 0)
    def _():
        pl.semaphore_wait(barrier, lower)

    def tell_ready(step):
        other_row = col * blocks + step // 2
        other_col = step % 2

        @pl.when(2 * other_row + other_col < rank)
        def _():
            pl.semaphore_signal(
                ready_sem.at[row],
                1,
                device_id={"row": other_row, "col": other_col},
                device_id_type=MESH,
            )

    @pl.when(col == 1)
    def _():
        pl.semaphore_signal(
            left_ready_sem, 1, device_id={"row": row, "col": 1 - col}, device_id_type=MESH
        )

    loop(2 * blocks, tell_ready)

    for load in loads[:5]:
        load.wait()
    normed = normalise(
        pair[...].reshape(flat, channels).astype(jnp.float32), vectors[0], vectors[1]
    ).astype(jnp.bfloat16)

    def project(index):
        return jnp.dot(normed, weights[index], preferred_element_type=jnp.float32)

    def gated(gate, value):
        product = jax.nn.sigmoid(project(gate)) * project(value)
        return product.astype(jnp.bfloat16).reshape(row_count, col_count, channels)

    right_block = gated(0, 1)
    own_right[...] = right_block

    @pl.when(mine)
    def _():
        right_all[slot, col] = right_block

    def right_copy(target):
        return pltpu.make_async_remote_copy(
            src_ref=own_right,
            dst_ref=right_all.at[slot, col],
            send_sem=send_sem.at[target],
            recv_sem=recv_sem.at[slot, col],
            device_id={"row": target, "col": owner},
            device_id_type=MESH,
        )

    left_copy = pltpu.make_async_remote_copy(
        src_ref=left_both.at[col],
        dst_ref=left_both.at[col],
        send_sem=left_send_sem,
        recv_sem=left_recv_sem,
        device_id={"row": row, "col": 1 - col},
        device_id_type=MESH,
    )

    def send_lower(target):
        @pl.when(2 * target + owner < rank)
        def _():
            right_copy(target).start()

    def send_higher(target):
        @pl.when(2 * target + owner > rank)
        def _():
            pl.semaphore_wait(ready_sem.at[target], 1)
            right_copy(target).start()

    loop(rows, send_lower)

    for load in loads[5:]:
        load.wait()
    left_both[col] = gated(2, 3)
    gating = jax.nn.sigmoid(project(4))

    @pl.when(col == 0)
    def _():
        pl.semaphore_wait(left_ready_sem, 1)

    left_copy.start()
    loop(rows, send_higher)

    left_copy.wait_recv()

    def block_wait(step):
        block = step // 2
        half = step % 2

        @pl.when(jnp.logical_or(col * blocks + block != row, half != col))
        def _():
            pltpu.make_async_remote_copy(
                src_ref=own_right,
                dst_ref=right_all.at[block, half],
                send_sem=send_sem.at[0],
                recv_sem=recv_sem.at[block, half],
                device_id={"row": row, "col": 1 - col},
                device_id_type=MESH,
            ).wait_recv()

    def contract(block):
        for j in range(row_count):
            right0 = right_all[block, 0, j].astype(jnp.float32)
            right1 = right_all[block, 1, j].astype(jnp.float32)
            for i in range(row_count):
                terms = (
                    left_both[0, i].astype(jnp.float32) * right0
                    + left_both[1, i].astype(jnp.float32) * right1
                )
                triangle[i, pl.ds(block * row_count + j, 1), :] = jnp.sum(
                    terms, axis=0, keepdims=True
                )

    loop(2 * blocks, block_wait)
    loop(blocks, contract)

    middle = normalise(triangle[...].reshape(flat, channels), vectors[2], vectors[3])
    update = gating * jnp.dot(
        middle.astype(jnp.bfloat16), weights[5], preferred_element_type=jnp.float32
    )
    result_ref[...] = update.astype(jnp.bfloat16).reshape(row_count, col_count, channels)

    left_copy.wait_send()

    def drain(target):
        @pl.when(2 * target + owner != rank)
        def _():
            right_copy(target).wait_send()

    loop(rows, drain)


def solution(mesh):
    rows = mesh.shape["row"]

    def on_device(pair_repr, in_gain, in_bias, left_gate_w, left_w, right_gate_w, right_w, out_gate_w, mid_gain, mid_bias, out_w):
        row_count, col_count, channels = pair_repr.shape
        blocks = col_count // row_count
        hbm = pl.BlockSpec(memory_space=pltpu.HBM)
        return pl.pallas_call(
            functools.partial(kernel, rows),
            out_shape=pltpu.VMEM(pair_repr.shape, jnp.bfloat16),
            in_specs=[hbm] * 11,
            out_specs=pl.BlockSpec(memory_space=pltpu.VMEM),
            scratch_shapes=[
                pltpu.VMEM(pair_repr.shape, jnp.bfloat16),
                pltpu.VMEM((6, channels, channels), jnp.bfloat16),
                pltpu.VMEM((4, 1, channels), jnp.float32),
                pltpu.VMEM(pair_repr.shape, jnp.bfloat16),
                pltpu.VMEM((blocks, 2, row_count, col_count, channels), jnp.bfloat16),
                pltpu.VMEM((2, row_count, col_count, channels), jnp.bfloat16),
                pltpu.VMEM((row_count, col_count, channels), jnp.float32),
                pltpu.SemaphoreType.DMA((11,)),
                pltpu.SemaphoreType.DMA((rows,)),
                pltpu.SemaphoreType.DMA((blocks, 2)),
                pltpu.SemaphoreType.DMA,
                pltpu.SemaphoreType.DMA,
                pltpu.SemaphoreType.REGULAR((rows,)),
                pltpu.SemaphoreType.REGULAR,
            ],
            compiler_params=pltpu.CompilerParams(
                collective_id=0, has_side_effects=True
            ),
        )(
            pair_repr,
            in_gain.reshape(1, channels),
            in_bias.reshape(1, channels),
            left_gate_w,
            left_w,
            right_gate_w,
            right_w,
            out_gate_w,
            mid_gain.reshape(1, channels),
            mid_bias.reshape(1, channels),
            out_w,
        )

    in_specs = (P(("groups", "row"), "col", None),) + (P(),) * 10
    out_specs = P(("groups", "row"), "col", None)
    return jax.shard_map(
        on_device, mesh=mesh, in_specs=in_specs, out_specs=out_specs, check_vma=False
    )
```

```python
import functools

import jax
import jax.numpy as jnp
from jax import lax
from jax.experimental import pallas as pl
from jax.experimental.pallas import tpu as pltpu
from jax.sharding import PartitionSpec as P

MESH = pl.DeviceIdType.MESH


def normalise(values, gain, bias):
    average = jnp.mean(values, axis=-1, keepdims=True)
    centred = values - average
    variance = jnp.mean(centred * centred, axis=-1, keepdims=True)
    return centred * lax.rsqrt(variance + 1e-05) * gain + bias


def loop(count, body):
    if count <= 16:
        for step in range(count):
            body(step)
    else:

        def wrapped(step, carry):
            body(step)
            return carry

        lax.fori_loop(0, count, wrapped, 0)


def kernel(
    rows,
    pair_hbm,
    in_gain_hbm,
    in_bias_hbm,
    left_gate_hbm,
    left_hbm,
    right_gate_hbm,
    right_hbm,
    out_gate_hbm,
    mid_gain_hbm,
    mid_bias_hbm,
    out_hbm,
    result_ref,
    pair,
    weights,
    vectors,
    own_right,
    right_all,
    left_both,
    triangle,
    load_sem,
    send_sem,
    recv_sem,
    left_send_sem,
    left_recv_sem,
    ready_sem,
    left_ready_sem,
):
    row = lax.axis_index("row")
    col = lax.axis_index("col")
    row_count, col_count, channels = pair.shape
    blocks = col_count // row_count
    flat = row_count * col_count
    owner = row // blocks
    slot = row % blocks
    mine = owner == col

    sources = [
        (pair_hbm, pair),
        (in_gain_hbm, vectors.at[0]),
        (in_bias_hbm, vectors.at[1]),
        (right_gate_hbm, weights.at[0]),
        (right_hbm, weights.at[1]),
        (left_gate_hbm, weights.at[2]),
        (left_hbm, weights.at[3]),
        (out_gate_hbm, weights.at[4]),
        (out_hbm, weights.at[5]),
        (mid_gain_hbm, vectors.at[2]),
        (mid_bias_hbm, vectors.at[3]),
    ]
    loads = [
        pltpu.make_async_copy(source, target, load_sem.at[index])
        for index, (source, target) in enumerate(sources)
    ]
    rank = 2 * row + col
    barrier = pltpu.get_barrier_semaphore()

    def is_peer(other_row, other_col):
        return (other_col == owner) | (other_row // blocks == col) | (other_row == row)

    def greet(step):
        @pl.when(is_peer(step // 2, step % 2) & (step > rank))
        def _():
            pl.semaphore_signal(
                barrier, 1, device_id={"row": step // 2, "col": step % 2}, device_id_type=MESH
            )

    loop(2 * rows, greet)

    for load in loads[:5]:
        load.start()

    def count_lower(step, total):
        return total + jnp.where(is_peer(step // 2, step % 2) & (step < rank), 1, 0)

    lower = jnp.int32(0)
    if rows <= 8:
        for step in range(2 * rows):
            lower = count_lower(step, lower)
    else:
        lower = lax.fori_loop(0, 2 * rows, count_lower, lower)

    for load in loads[5:]:
        load.start()

    @pl.when(lower > 0)
    def _():
        pl.semaphore_wait(barrier, lower)

    def tell_ready(step):
        other_row = col * blocks + step // 2
        other_col = step % 2

        @pl.when(2 * other_row + other_col < rank)
        def _():
            pl.semaphore_signal(
                ready_sem.at[row],
                1,
                device_id={"row": other_row, "col": other_col},
                device_id_type=MESH,
            )

    @pl.when(col == 1)
    def _():
        pl.semaphore_signal(
            left_ready_sem, 1, device_id={"row": row, "col": 1 - col}, device_id_type=MESH
        )

    loop(2 * blocks, tell_ready)

    for load in loads[:5]:
        load.wait()
    normed = normalise(
        pair[...].reshape(flat, channels).astype(jnp.float32), vectors[0], vectors[1]
    ).astype(jnp.bfloat16)

    def project(index):
        return jnp.dot(normed, weights[index], preferred_element_type=jnp.float32)

    def gated(gate, value):
        product = jax.nn.sigmoid(project(gate)) * project(value)
        return product.astype(jnp.bfloat16).reshape(row_count, col_count, channels)

    right_block = gated(0, 1)
    own_right[...] = right_block

    @pl.when(mine)
    def _():
        right_all[slot, col] = right_block

    def right_copy(target):
        return pltpu.make_async_remote_copy(
            src_ref=own_right,
            dst_ref=right_all.at[slot, col],
            send_sem=send_sem.at[target],
            recv_sem=recv_sem.at[slot, col],
            device_id={"row": target, "col": owner},
            device_id_type=MESH,
        )

    left_copy = pltpu.make_async_remote_copy(
        src_ref=left_both.at[col],
        dst_ref=left_both.at[col],
        send_sem=left_send_sem,
        recv_sem=left_recv_sem,
        device_id={"row": row, "col": 1 - col},
        device_id_type=MESH,
    )

    def send_lower(target):
        @pl.when(2 * target + owner < rank)
        def _():
            right_copy(target).start()

    def send_higher(target):
        @pl.when(2 * target + owner > rank)
        def _():
            pl.semaphore_wait(ready_sem.at[target], 1)
            right_copy(target).start()

    loop(rows, send_lower)

    for load in loads[5:]:
        load.wait()
    left_both[col] = gated(2, 3)
    gating = jax.nn.sigmoid(project(4))

    @pl.when(col == 0)
    def _():
        pl.semaphore_wait(left_ready_sem, 1)

    left_copy.start()
    loop(rows, send_higher)

    left_copy.wait_recv()

    def block_wait(step):
        block = step // 2
        half = step % 2

        @pl.when(jnp.logical_or(col * blocks + block != row, half != col))
        def _():
            pltpu.make_async_remote_copy(
                src_ref=own_right,
                dst_ref=right_all.at[block, half],
                send_sem=send_sem.at[0],
                recv_sem=recv_sem.at[block, half],
                device_id={"row": row, "col": 1 - col},
                device_id_type=MESH,
            ).wait_recv()

    def contract(block):
        for j in range(row_count):
            right0 = right_all[block, 0, j].astype(jnp.float32)
            right1 = right_all[block, 1, j].astype(jnp.float32)
            for i in range(row_count):
                terms = (
                    left_both[0, i].astype(jnp.float32) * right0
                    + left_both[1, i].astype(jnp.float32) * right1
                )
                triangle[i, pl.ds(block * row_count + j, 1), :] = jnp.sum(
                    terms, axis=0, keepdims=True
                )

    def finish(block):
        block_wait(2 * block)
        block_wait(2 * block + 1)
        contract(block)

    loop(blocks, finish)

    middle = normalise(triangle[...].reshape(flat, channels), vectors[2], vectors[3])
    update = gating * jnp.dot(
        middle.astype(jnp.bfloat16), weights[5], preferred_element_type=jnp.float32
    )
    result_ref[...] = update.astype(jnp.bfloat16).reshape(row_count, col_count, channels)

    left_copy.wait_send()

    def drain(target):
        @pl.when(2 * target + owner != rank)
        def _():
            right_copy(target).wait_send()

    loop(rows, drain)


def solution(mesh):
    rows = mesh.shape["row"]

    def on_device(pair_repr, in_gain, in_bias, left_gate_w, left_w, right_gate_w, right_w, out_gate_w, mid_gain, mid_bias, out_w):
        row_count, col_count, channels = pair_repr.shape
        blocks = col_count // row_count
        hbm = pl.BlockSpec(memory_space=pltpu.HBM)
        return pl.pallas_call(
            functools.partial(kernel, rows),
            out_shape=pltpu.VMEM(pair_repr.shape, jnp.bfloat16),
            in_specs=[hbm] * 11,
            out_specs=pl.BlockSpec(memory_space=pltpu.VMEM),
            scratch_shapes=[
                pltpu.VMEM(pair_repr.shape, jnp.bfloat16),
                pltpu.VMEM((6, channels, channels), jnp.bfloat16),
                pltpu.VMEM((4, 1, channels), jnp.float32),
                pltpu.VMEM(pair_repr.shape, jnp.bfloat16),
                pltpu.VMEM((blocks, 2, row_count, col_count, channels), jnp.bfloat16),
                pltpu.VMEM((2, row_count, col_count, channels), jnp.bfloat16),
                pltpu.VMEM((row_count, col_count, channels), jnp.float32),
                pltpu.SemaphoreType.DMA((11,)),
                pltpu.SemaphoreType.DMA((rows,)),
                pltpu.SemaphoreType.DMA((blocks, 2)),
                pltpu.SemaphoreType.DMA,
                pltpu.SemaphoreType.DMA,
                pltpu.SemaphoreType.REGULAR((rows,)),
                pltpu.SemaphoreType.REGULAR,
            ],
            compiler_params=pltpu.CompilerParams(
                collective_id=0, has_side_effects=True
            ),
        )(
            pair_repr,
            in_gain.reshape(1, channels),
            in_bias.reshape(1, channels),
            left_gate_w,
            left_w,
            right_gate_w,
            right_w,
            out_gate_w,
            mid_gain.reshape(1, channels),
            mid_bias.reshape(1, channels),
            out_w,
        )

    in_specs = (P(("groups", "row"), "col", None),) + (P(),) * 10
    out_specs = P(("groups", "row"), "col", None)
    return jax.shard_map(
        on_device, mesh=mesh, in_specs=in_specs, out_specs=out_specs, check_vma=False
    )
```
